32 devices in a mesh: outer: 4 (over x, core), inner: 8 (over z, y).
Axes of the slice: x: 2, y: 2, z: 4, core: 2. Of those that a mesh axis runs over, the one named last changes fastest.
Arguments:
- vertex: float32 [131072, 128], P(('outer', 'inner')), may hold values from -1.75 to 1.75
- context: float32 [65536, 128], P(('outer', 'inner')), may hold values from -1.75 to 1.75
- tile_count: int32 [128], P(('outer', 'inner')), may hold values from 1 to 8, as said below
- tile_vert: int32 [128, 8], P(('outer', 'inner')), may hold values from 0 to 15
- tile_context: int32 [128, 8], P(('outer', 'inner')), may hold values from 0 to 7
- positives: int32 [128, 8, 256], P(('outer', 'inner')), may hold values from 0 to 255
- negatives: int32 [128, 8, 4, 256], P(('outer', 'inner')), may hold values from 0 to 255
Outputs:
- vertex_out: float32 [131072, 128], P(('outer', 'inner'))
- context_out: float32 [65536, 128], P(('outer', 'inner'))
The draws below stay inside these ranges and needn't reach their ends.
Inputs may be any that keep to these rules, and one draw needn't show every extreme that they name: `tile_count`: every entry is at least 1, and in every tour step some device has all 8 slots live.
All inputs are finite; a program needn't handle non-finite values.
Results may differ from the reference program's by a relative error of at most 0.0003.
Values sent between devices are 32-bit elements; how exact they have to be, the bound alone decides.
A program may use at most 64 MiB of HBM per device.

```python
import jax
import jax.numpy as jnp
from jax import lax

D = 128
TILE = 256
VROWS = 4096
CROWS = 2048
STEPS = 4
SLOTS = 8
NEG = 4
LISTS = 128
VTOTAL = 131072
CTOTAL = 65536
N_OUTER = 4
N_INNER = 8


def draw_tile_count(key, part):
    members = LISTS // STEPS
    counts = jax.random.randint(key, (members, STEPS), 1, SLOTS)
    chosen = jax.random.randint(jax.random.fold_in(key, 7), (STEPS,), 0, members)
    counts = counts.at[chosen, jnp.arange(STEPS)].set(SLOTS)
    return counts.reshape(LISTS).astype(jnp.int32)


def with_ends(entries, own_key, least, largest):
    dims = entries.shape
    spot = [jax.random.randint(jax.random.fold_in(own_key, axis), (), 0, dims[axis]) for axis in range(len(dims))]
    entries = entries.at[tuple(spot)].set(least)
    longest = dims.index(max(dims))
    spot[longest] = (spot[longest] + 1) % dims[longest]
    return entries.at[tuple(spot)].set(largest)


def levels(own_key, dims, split, smallest, top_value):
    def one(axis_at, parts):
        heights = jax.random.uniform(jax.random.fold_in(jax.random.fold_in(own_key, 6), axis_at), (parts,), jnp.float32, smallest / len(split), top_value / len(split))
        return jnp.repeat(jnp.exp(heights), dims[axis_at] // parts).reshape((-1,) + (1,) * (len(dims) - axis_at - 1))

    level = one(*split[0])
    for cut in split[1:]:
        level = level * one(*cut)
    return level


def centred(key, extent, spread, most, split=(), kind=jnp.bfloat16):
    gain = levels(key, extent, split, -0.22, 0.18) if split else 1.0
    entries = jax.random.normal(key, extent, jnp.float32) * spread * gain
    return jnp.minimum(jnp.maximum(entries, -most), most).astype(kind)


def setup_inputs(seed: int = 0) -> dict:
    key_of = jax.random.split(jax.random.key(seed), 8)
    return {
        "vertex": centred(key_of[0], (VTOTAL, D), 0.3, 1.75, ((0, 32),), jnp.float32),
        "context": centred(key_of[1], (CTOTAL, D), 0.3, 1.75, ((0, 32),), jnp.float32),
        "tile_count": draw_tile_count(jax.random.fold_in(key_of[7], 71), 0),
        "tile_vert": with_ends(jax.random.randint(key_of[3], (LISTS, SLOTS), 0, VROWS // TILE), jax.random.fold_in(key_of[3], 1), 0, (VROWS // TILE) - 1).astype(jnp.int32),
        "tile_context": with_ends(jax.random.randint(key_of[4], (LISTS, SLOTS), 0, CROWS // TILE), jax.random.fold_in(key_of[4], 1), 0, (CROWS // TILE) - 1).astype(jnp.int32),
        "positives": with_ends(jax.random.randint(key_of[5], (LISTS, SLOTS, TILE), 0, TILE), jax.random.fold_in(key_of[5], 1), 0, TILE - 1).astype(jnp.int32),
        "negatives": with_ends(jax.random.randint(key_of[6], (LISTS, SLOTS, NEG, TILE), 0, TILE), jax.random.fold_in(key_of[6], 1), 0, TILE - 1).astype(jnp.int32),
    }


learn_rate = 0.5


def train_rows(visiting, resident, count, tile_vert, tile_context, positives, negatives):
    slots = tile_vert.shape[0]
    width = visiting.shape[1]
    offsets = jnp.arange(TILE, dtype=jnp.int32)
    row_index = tile_vert[:, None] * TILE + offsets[None, :]
    pos_index = tile_context[:, None] * TILE + positives
    neg_index = tile_context[:, None, None] * TILE + negatives
    live = (jnp.arange(slots, dtype=jnp.int32) < count).astype(jnp.float32)
    anchor = visiting[row_index]
    pos_rows = resident[pos_index]
    neg_rows = resident[neg_index]
    pos_score = jnp.sum(anchor * pos_rows, -1)
    neg_score = jnp.sum(anchor[:, None] * neg_rows, -1)
    pos_grad = (jax.nn.sigmoid(pos_score) - 1.0) * live[:, None]
    neg_grad = jax.nn.sigmoid(neg_score) * live[:, None, None]
    vert_delta = pos_grad[..., None] * pos_rows + jnp.sum(neg_grad[..., None] * neg_rows, 1)
    vert_total = jnp.zeros_like(visiting).at[row_index.reshape(-1)].add(vert_delta.reshape(-1, width))
    context_total = jnp.zeros_like(resident).at[pos_index.reshape(-1)].add((pos_grad[..., None] * anchor).reshape(-1, width))
    context_total = context_total.at[neg_index.reshape(-1)].add((neg_grad[..., None] * anchor[:, None]).reshape(-1, width))
    return visiting - learn_rate * vert_total, resident - learn_rate * context_total


def apply_lists(operands):
    return train_rows(*operands)


def reference(vertex, context, tile_count, tile_vert, tile_context, positives, negatives):
    members = N_OUTER * N_INNER
    visiting = vertex.reshape(members, VROWS, D)
    resident = context.reshape(members, CROWS, D)
    counts = tile_count.reshape(members, STEPS)
    vert_lists = tile_vert.reshape(members, STEPS, SLOTS)
    context_lists = tile_context.reshape(members, STEPS, SLOTS)
    pos_lists = positives.reshape(members, STEPS, SLOTS, TILE)
    neg_lists = negatives.reshape(members, STEPS, SLOTS, NEG, TILE)
    for number in range(STEPS):
        visiting, resident = lax.map(apply_lists, (visiting, resident, counts[:, number], vert_lists[:, number], context_lists[:, number], pos_lists[:, number], neg_lists[:, number]))
        if number + 1 < STEPS:
            visiting = jnp.roll(visiting.reshape(N_OUTER, N_INNER, VROWS, D), 1, axis=1).reshape(members, VROWS, D)
    visiting = jnp.roll(visiting.reshape(N_OUTER, N_INNER, VROWS, D), 1, axis=0)
    return visiting.reshape(VTOTAL, D), resident.reshape(CTOTAL, D)
```

```python
import functools

import jax
import jax.numpy as jnp
from jax import lax
from jax.experimental import pallas as pl
from jax.experimental.pallas import tpu as pltpu
from jax.sharding import PartitionSpec as P

TILE = 256

learn_rate = 0.5

MESH = pl.DeviceIdType.MESH


def halves(x):
    high = x.astype(jnp.bfloat16)
    low = (x - high.astype(jnp.float32)).astype(jnp.bfloat16)
    return high, low


def dot(a, b, dims):
    return lax.dot_general(a, b, (dims, ((), ())), preferred_element_type=jnp.float32)


class Fields:
    def __init__(self, tiles, slots, ctiles):
        start = 0
        for name, size in (
            ("place", tiles), ("order", tiles), ("last", tiles), ("spot", slots), ("prev", slots),
            ("lastspot", slots), ("vert", slots), ("context", slots), ("prevc", slots),
            ("lastc", ctiles), ("count", 1),
        ):
            setattr(self, name, start)
            start += size
        self.width = -(-start // 128) * 128


def tables(tile_count, tile_vert, tile_context, tiles, ctiles):
    steps, slots = tile_vert.shape
    i32 = jnp.int32
    ks = jnp.arange(tiles, dtype=i32)
    cs = jnp.arange(ctiles, dtype=i32)
    ts = jnp.arange(slots, dtype=i32)
    is_tile = tile_vert[:, :, None] == ks
    marked = jnp.any(is_tile, 1).astype(i32)
    before = jnp.sum(jnp.where(ks[None, :, None] > ks[None, None, :], marked[:, None, :], 0), -1)
    total = jnp.sum(marked, -1, keepdims=True)
    place = jnp.where(marked == 1, before, total + ks - before)
    order = jnp.sum(jnp.where(place[:, None, :] == ks[None, :, None], ks, 0), -1)
    last = jnp.max(jnp.where(is_tile, ts[None, :, None], -1), 1)
    spot = jnp.sum(jnp.where(is_tile, place[:, None, :], 0), -1)
    earlier = ts[None, :, None] > ts[None, None, :]
    prev = jnp.max(jnp.where(earlier & (tile_vert[:, :, None] == tile_vert[:, None, :]), ts, -1), -1)
    lastspot = jnp.max(jnp.where(spot[:, None, :] == ts[None, :, None], ts, -1), -1)
    prevc = jnp.max(jnp.where(earlier & (tile_context[:, :, None] == tile_context[:, None, :]), ts, -1), -1)
    lastc = jnp.max(jnp.where(tile_context[:, None, :] == cs[None, :, None], ts, -1), -1)
    rows = jnp.concatenate(
        [place, order, last, spot, prev, lastspot, tile_vert, tile_context, prevc, lastc, tile_count[:, None]], 1
    )
    width = Fields(tiles, slots, ctiles).width
    return jnp.pad(rows, ((0, -steps % 8), (0, width - rows.shape[1])))


def kernel(
    sizes, meta, meta_s, vertex, context, positives, negatives, v_out, c_out,
    pool0, pool1, pool2, pool3, cpool0, cpool1, cpool2, cpool3,
    near0, far0, near1, near2, far2, near3, csend0, csend2, last, out,
    lists_v, lists, pos_home, neg_home, pos_role, neg_role, send, recv, local,
):
    tiles, slots, ctiles = sizes
    f = Fields(tiles, slots, ctiles)
    outer, inner = lax.axis_size("outer"), lax.axis_size("inner")
    o, i = lax.axis_index("outer"), lax.axis_index("inner")

    def swapped(o, i):
        return 2 * (o // 2) + i % 2, 2 * (i // 2) + o % 2

    def at(o, i):
        return (o + outer) % outer, (i + inner) % inner

    ro, ri = swapped(o, i)
    stays = o % 2 == i % 2

    def remote(source, target, k, device):
        return pltpu.make_async_remote_copy(
            src_ref=source, dst_ref=target, send_sem=send.at[k], recv_sem=recv.at[k],
            device_id=device, device_id_type=MESH,
        )

    here = [
        pltpu.make_async_copy(vertex, pool0.at[pl.ds(0, tiles)], local.at[0]),
        pltpu.make_async_copy(context, cpool0.at[pl.ds(0, ctiles)], local.at[1]),
        pltpu.make_async_copy(positives.at[pl.ds(0, 1)], pos_home.at[pl.ds(0, 1)], local.at[2]),
        pltpu.make_async_copy(negatives.at[pl.ds(0, 1)], neg_home.at[pl.ds(0, 1)], local.at[3]),
        pltpu.make_async_copy(positives.at[pl.ds(3, 1)], pos_home.at[pl.ds(1, 1)], local.at[4]),
        pltpu.make_async_copy(negatives.at[pl.ds(3, 1)], neg_home.at[pl.ds(1, 1)], local.at[5]),
    ]
    for copy in here:
        copy.start()

    sends = [
        remote(meta, lists_v.at[1], 1, at(o, i - 1)),
        remote(meta, lists_v.at[2], 2, swapped(*at(o, i + 1))),
        remote(meta, lists_v.at[3], 3, swapped(*at(o, i - 1))),
        remote(meta, lists_v.at[4], 4, at(o + 1, i)),
    ]
    for copy in sends:
        copy.start()
    role_copies = [
        remote(meta, lists_v.at[0], 0, (ro, ri)),
        remote(positives.at[pl.ds(1, 2)], pos_role, 5, (ro, ri)),
        remote(negatives.at[pl.ds(1, 2)], neg_role, 6, (ro, ri)),
    ]
    own_copies = [
        pltpu.make_async_copy(meta, lists_v.at[0], local.at[6]),
        pltpu.make_async_copy(positives.at[pl.ds(1, 2)], pos_role, local.at[7]),
        pltpu.make_async_copy(negatives.at[pl.ds(1, 2)], neg_role, local.at[8]),
    ]

    @pl.when(stays)
    def _():
        for copy in own_copies:
            copy.start()

    @pl.when(jnp.logical_not(stays))
    def _():
        for copy in role_copies:
            copy.start()

    rows = lax.broadcasted_iota(jnp.int32, (TILE, TILE), 0)
    group = 2 if slots % 2 == 0 else 1
    width = pool0.shape[-1]

    def train(count, vert_at, prev_at, context_at, prevc_at, step, pos, neg, pool, held, cpool):
        def slot_group(g, carry):
            work = []
            for j in range(group):
                t = g * group + j
                live = (t < count).astype(jnp.float32)
                work.append((t, vert_at(t), context_at(t), live))
            anchors = [halves(pool[w[1]]) for w in work]
            partners = [halves(cpool[w[2]]) for w in work]
            gradients = []
            for (t, _, _, live), (a_high, a_low), (p_high, p_low) in zip(work, anchors, partners):
                both = jnp.concatenate([a_high, a_low], 1)
                twice = jnp.concatenate([p_high, p_high], 1)
                scores = dot(twice, both, ((1,), (1,))) + dot(p_low, a_high, ((1,), (1,)))
                half = -0.5 * learn_rate * live
                change = half * jnp.tanh(0.5 * scores) + half
                gradient = jnp.where(pos[step, pl.ds(t, 1)] == rows, change + learn_rate * live, 0.0)
                for k in range(neg.shape[2]):
                    gradient += jnp.where(neg[step, t, pl.ds(k, 1)] == rows, change, 0.0)
                gradients.append(halves(gradient))
            for (t, at_v, at_c, _), (a_high, a_low), (p_high, p_low), (g_high, g_low) in zip(
                work, anchors, partners, gradients
            ):
                wide = dot(g_high, jnp.concatenate([p_high, p_low], 1), ((0,), (0,)))
                prev = prev_at(t)
                base = pool[jnp.where(prev < 0, at_v, held + prev)]
                pool[held + t] = base + (wide[:, :width] + wide[:, width:] + dot(g_low, p_high, ((0,), (0,))))
                wide = dot(g_high, jnp.concatenate([a_high, a_low], 1), ((1,), (0,)))
                prev = prevc_at(t)
                base = cpool[jnp.where(prev < 0, at_c, ctiles + prev)]
                cpool[ctiles + t] = base + (wide[:, :width] + wide[:, width:] + dot(g_low, a_high, ((1,), (0,))))
            return carry

        lax.fori_loop(0, slots // group, slot_group, 0)

    def pack(source, targets, index):
        p = 0
        for target, size in targets:
            for k in range(size):
                target[k] = source[index(p)]
                p += 1

    def context_index(row):
        def index(k):
            slot = row(f.lastc + k)
            return jnp.where(slot < 0, k, ctiles + slot)
        return index

    def mine(s):
        return lambda k: meta_s[s, k]

    def other(which, s):
        return lambda k: lists[which, s, k]

    for copy in here[:4]:
        copy.wait()
    m = mine(0)
    train(
        m(f.count), lambda t: m(f.vert + t), lambda t: m(f.prev + t), lambda t: m(f.context + t),
        lambda t: m(f.prevc + t), 0, pos_home, neg_home, pool0, tiles, cpool0,
    )
    for copy in sends:
        copy.wait()

    @pl.when(stays)
    def _():
        for copy in own_copies:
            copy.wait()

    @pl.when(jnp.logical_not(stays))
    def _():
        for copy in role_copies:
            copy.wait()

    to_smem = pltpu.make_async_copy(lists_v, lists, local.at[9])
    to_smem.start()
    to_smem.wait()

    after = other(1, 1)

    def index0(p):
        tile = after(f.order + p)
        slot = m(f.last + tile)
        return jnp.where(slot < 0, tile, tiles + slot)

    pack(pool0, ((near0, slots),), index0)
    send_near0 = remote(near0, pool1.at[pl.ds(0, slots)], 7, swapped(*at(o, i + 1)))
    send_near0.start()
    pack(cpool0, ((csend0, ctiles),), context_index(m))
    send_c0 = remote(csend0, cpool1.at[pl.ds(0, ctiles)], 8, (ro, ri))
    keep_c0 = pltpu.make_async_copy(csend0, cpool1.at[pl.ds(0, ctiles)], local.at[10])

    @pl.when(stays)
    def _():
        keep_c0.start()

    @pl.when(jnp.logical_not(stays))
    def _():
        send_c0.start()

    pack(pool0, ((far0, tiles - slots),), lambda p: index0(slots + p))
    send_far0 = remote(far0, pool2.at[pl.ds(slots, tiles - slots)], 9, swapped(*at(o, i + 2)))
    send_far0.start()

    send_near0.wait()

    @pl.when(stays)
    def _():
        keep_c0.wait()

    @pl.when(jnp.logical_not(stays))
    def _():
        send_c0.wait()

    r = other(0, 1)
    train(
        r(f.count), lambda t: r(f.spot + t), lambda t: r(f.prev + t), lambda t: r(f.context + t),
        lambda t: r(f.prevc + t), 0, pos_role, neg_role, pool1, slots, cpool1,
    )

    def index1(p):
        slot = r(f.lastspot + p)
        return jnp.where(slot < 0, p, slots + slot)

    pack(pool1, ((near1, slots),), index1)
    send_near1 = remote(near1, pool2.at[pl.ds(0, slots)], 10, swapped(*at(ro, ri + 1)))
    send_near1.start()
    pack(cpool1, ((cpool2, ctiles),), context_index(r))

    send_near1.wait()
    send_far0.wait()
    r2 = other(0, 2)
    before = other(2, 1)
    train(
        r2(f.count), lambda t: before(f.place + r2(f.vert + t)), lambda t: r2(f.prev + t),
        lambda t: r2(f.context + t), lambda t: r2(f.prevc + t), 1, pos_role, neg_role, pool2, tiles, cpool2,
    )
    following = other(3, 3)

    def index2(p):
        tile = following(f.order + p)
        slot = r2(f.last + tile)
        return jnp.where(slot < 0, before(f.place + tile), tiles + slot)

    pack(pool2, ((near2, slots),), index2)
    send_near2 = remote(near2, pool3.at[pl.ds(0, slots)], 11, at(ro, ri + 1))
    send_near2.start()
    pack(cpool2, ((csend2, ctiles),), context_index(r2))
    send_c2 = remote(csend2, cpool3.at[pl.ds(0, ctiles)], 12, (ro, ri))
    keep_c2 = pltpu.make_async_copy(csend2, cpool3.at[pl.ds(0, ctiles)], local.at[11])

    @pl.when(stays)
    def _():
        keep_c2.start()

    @pl.when(jnp.logical_not(stays))
    def _():
        send_c2.start()

    pack(pool2, ((far2, tiles - slots),), lambda p: index2(slots + p))
    send_far2 = remote(far2, last.at[pl.ds(slots, tiles - slots)], 13, at(ro + 1, ri + 1))
    send_far2.start()

    for copy in here[4:]:
        copy.wait()
    send_near2.wait()

    @pl.when(stays)
    def _():
        keep_c2.wait()

    @pl.when(jnp.logical_not(stays))
    def _():
        send_c2.wait()

    m3 = mine(3)
    train(
        m3(f.count), lambda t: m3(f.spot + t), lambda t: m3(f.prev + t), lambda t: m3(f.context + t),
        lambda t: m3(f.prevc + t), 1, pos_home, neg_home, pool3, slots, cpool3,
    )

    def index3(p):
        slot = m3(f.lastspot + p)
        return jnp.where(slot < 0, p, slots + slot)

    pack(pool3, ((near3, slots),), index3)
    send_near3 = remote(near3, last.at[pl.ds(0, slots)], 14, at(o + 1, i))
    send_near3.start()
    pack(cpool3, ((csend0, ctiles),), context_index(m3))
    put_c = pltpu.make_async_copy(csend0, c_out, local.at[12])
    put_c.start()
    send_far2.wait()
    send_near3.wait()
    final = other(4, 3)
    pack(last, ((out, tiles),), lambda k: final(f.place + k))
    put_v = pltpu.make_async_copy(out, v_out, local.at[13])
    put_v.start()
    put_c.wait()
    put_v.wait()


ANY = pl.BlockSpec(memory_space=pl.ANY)
SMEM = pl.BlockSpec(memory_space=pltpu.SMEM)
VMEM = pl.BlockSpec(memory_space=pltpu.VMEM)


def body(vertex, context, tile_count, tile_vert, tile_context, positives, negatives):
    steps, slots = tile_vert.shape
    width = vertex.shape[1]
    tiles, ctiles = vertex.shape[0] // TILE, context.shape[0] // TILE
    f32, i32 = jnp.float32, jnp.int32
    meta = tables(tile_count, tile_vert, tile_context, tiles, ctiles)
    v = vertex.reshape(tiles, TILE, width)
    c = context.reshape(ctiles, TILE, width)

    def block(n):
        return pltpu.VMEM((n, TILE, width), f32)

    far = tiles - slots
    scratch = [
        block(tiles + slots), block(2 * slots), block(tiles + slots), block(2 * slots),
        *[block(ctiles + slots)] * 4,
        block(slots), block(far), block(slots), block(slots), block(far), block(slots),
        block(ctiles), block(ctiles), block(tiles), block(tiles),
        pltpu.VMEM((5,) + meta.shape, i32), pltpu.SMEM((5,) + meta.shape, i32),
        *[pltpu.VMEM((2,) + positives.shape[1:], i32), pltpu.VMEM((2,) + negatives.shape[1:], i32)] * 2,
        pltpu.SemaphoreType.DMA((15,)), pltpu.SemaphoreType.DMA((15,)), pltpu.SemaphoreType.DMA((14,)),
    ]
    v, c = pl.pallas_call(
        functools.partial(kernel, (tiles, slots, ctiles)),
        out_shape=(jax.ShapeDtypeStruct(v.shape, f32), jax.ShapeDtypeStruct(c.shape, f32)),
        in_specs=[VMEM, SMEM] + [ANY] * 4,
        out_specs=(ANY, ANY),
        scratch_shapes=scratch,
        compiler_params=pltpu.CompilerParams(has_side_effects=True, vmem_limit_bytes=60 * 1024 * 1024),
    )(meta, meta, v, c, positives, negatives)
    return v.reshape(vertex.shape), c.reshape(context.shape)


def solution(mesh):
    lists = P(("outer", "inner"))
    rows = P(("outer", "inner"), None)
    return jax.shard_map(
        body,
        mesh=mesh,
        in_specs=(
            rows, rows, lists, rows, rows,
            P(("outer", "inner"), None, None), P(("outer", "inner"), None, None, None),
        ),
        out_specs=(rows, rows),
        check_vma=False,
    )
```

```python
import functools

import jax
import jax.numpy as jnp
from jax import lax
from jax.experimental import pallas as pl
from jax.experimental.pallas import tpu as pltpu
from jax.sharding import PartitionSpec as P

TILE = 256

learn_rate = 0.5

MESH = pl.DeviceIdType.MESH


def halves(x):
    high = x.astype(jnp.bfloat16)
    low = (x - high.astype(jnp.float32)).astype(jnp.bfloat16)
    return high, low


def dot(a, b, dims):
    return lax.dot_general(a, b, (dims, ((), ())), preferred_element_type=jnp.float32)


class Fields:
    def __init__(self, tiles, slots, ctiles):
        start = 0
        for name, size in (
            ("place", tiles), ("order", tiles), ("last", tiles), ("spot", slots), ("prev", slots),
            ("lastspot", slots), ("vert", slots), ("context", slots), ("prevc", slots),
            ("lastc", ctiles), ("count", 1),
        ):
            setattr(self, name, start)
            start += size
        self.width = -(-start // 128) * 128


def tables(f, tiles, slots, ctiles, count, vert, context):
    steps = vert.shape[0]
    shape = (steps, f.width)
    col = lax.broadcasted_iota(jnp.int32, shape, 1)
    row = lax.broadcasted_iota(jnp.int32, shape, 0)
    v = [jnp.broadcast_to(vert[:, t : t + 1], shape) for t in range(slots)]
    c = [jnp.broadcast_to(context[:, t : t + 1], shape) for t in range(slots)]

    def latest(values, at, upto=slots):
        found = jnp.full(shape, -1, jnp.int32)
        for t in range(upto):
            found = jnp.where(values[t] == at, t, found)
        return found

    first = [jnp.where(latest(v, v[t], t) < 0, 1, 0) for t in range(slots)]
    total = functools.reduce(lambda x, y: x + y, first)

    def before(at):
        return functools.reduce(lambda x, y: x + y, [jnp.where(v[t] < at, first[t], 0) for t in range(slots)])

    def place(at):
        count_before = before(at)
        return jnp.where(latest(v, at) >= 0, count_before, total + at - count_before)

    order = jnp.zeros(shape, jnp.int32)
    for k in range(tiles):
        order = jnp.where(place(jnp.full(shape, k, jnp.int32)) == col - f.order, k, order)
    out = jnp.zeros(shape, jnp.int32)

    def put(start, size, value):
        return jnp.where((col >= start) & (col < start + size), value, out)

    out = put(f.place, tiles, place(col - f.place))
    out = put(f.order, tiles, order)
    out = put(f.last, tiles, latest(v, col - f.last))
    spots = [before(v[t]) for t in range(slots)]
    out = put(f.lastspot, slots, latest(spots, col - f.lastspot))
    out = put(f.lastc, ctiles, latest(c, col - f.lastc))
    for t in range(slots):
        out = put(f.spot + t, 1, spots[t])
        out = put(f.prev + t, 1, latest(v, v[t], t))
        out = put(f.prevc + t, 1, latest(c, c[t], t))
        out = put(f.vert + t, 1, v[t])
        out = put(f.context + t, 1, c[t])
    for s in range(steps):
        out = jnp.where((row == s) & (col == f.count), count[s], out)
    return out


def kernel(
    sizes, tile_count, tile_vert, tile_context, vertex, context, positives, negatives, v_out, c_out,
    pool0, pool1, pool2, pool3, cpool0, cpool1, cpool2, cpool3,
    near0, far0, near1, near2, far2, near3, csend0, csend2, last, out,
    relay_a, relay_b, relay_c, vert_v, context_v, meta, meta_s, lists_v, lists, pos_home, neg_home, pos_role, neg_role, send, recv, local,
):
    tiles, slots, ctiles = sizes
    f = Fields(tiles, slots, ctiles)
    outer, inner = lax.axis_size("outer"), lax.axis_size("inner")
    o, i = lax.axis_index("outer"), lax.axis_index("inner")

    def swapped(o, i):
        return 2 * (o // 2) + i % 2, 2 * (i // 2) + o % 2

    def at(o, i):
        return (o + outer) % outer, (i + inner) % inner

    ro, ri = swapped(o, i)
    stays = o % 2 == i % 2

    pair = (o % 2, i % 2)

    def when(*kinds):
        ok = [(pair[0] == a) & (pair[1] == b) for a, b in kinds]
        return pl.when(functools.reduce(jnp.logical_or, ok))

    def remote(source, target, k, device, into=None):
        return pltpu.make_async_remote_copy(
            src_ref=source, dst_ref=target, send_sem=send.at[k], recv_sem=recv.at[k if into is None else into],
            device_id=device, device_id_type=MESH,
        )

    load = [
        pltpu.make_async_copy(tile_vert, vert_v, local.at[14]),
        pltpu.make_async_copy(tile_context, context_v, local.at[15]),
    ]
    for copy in load:
        copy.start()

    here = [
        pltpu.make_async_copy(vertex, pool0.at[pl.ds(0, tiles)], local.at[0]),
        pltpu.make_async_copy(context, cpool0.at[pl.ds(0, ctiles)], local.at[1]),
        pltpu.make_async_copy(positives.at[pl.ds(0, 1)], pos_home.at[pl.ds(0, 1)], local.at[2]),
        pltpu.make_async_copy(negatives.at[pl.ds(0, 1)], neg_home.at[pl.ds(0, 1)], local.at[3]),
        pltpu.make_async_copy(positives.at[pl.ds(3, 1)], pos_home.at[pl.ds(1, 1)], local.at[4]),
        pltpu.make_async_copy(negatives.at[pl.ds(3, 1)], neg_home.at[pl.ds(1, 1)], local.at[5]),
    ]
    for copy in here:
        copy.start()

    barrier = pltpu.get_barrier_semaphore()
    sources = [
        at(o, i + 1), (ro, ri - 1), (ro, ri + 1), at(o - 1, i), swapped(*at(ro, ri - 1)),
        swapped(*at(o, i - 1)), swapped(*at(o - 1, i - 1)), at(o, i - 2), at(o - 2, i),
    ]
    for source in sources:
        pl.semaphore_signal(barrier, inc=1, device_id=at(*source), device_id_type=MESH)

    @pl.when(jnp.logical_not(stays))
    def _():
        pl.semaphore_signal(barrier, inc=1, device_id=(ro, ri), device_id_type=MESH)

    for copy in load:
        copy.wait()
    meta[...] = jnp.zeros_like(meta)
    meta[pl.ds(0, vert_v.shape[0])] = tables(f, tiles, slots, ctiles, tile_count, vert_v, context_v)
    own_meta = pltpu.make_async_copy(meta, meta_s, local.at[16])
    own_meta.start()

    @pl.when(stays)
    def _():
        pl.semaphore_wait(barrier, len(sources))

    @pl.when(jnp.logical_not(stays))
    def _():
        pl.semaphore_wait(barrier, len(sources) + 1)

    sends = [
        remote(meta, lists_v.at[1], 1, at(o, i - 1)),
        remote(meta, lists_v.at[2], 2, swapped(*at(o, i + 1))),
        remote(meta, lists_v.at[3], 3, swapped(*at(o, i - 1))),
        remote(meta, lists_v.at[4], 4, at(o + 1, i)),
    ]
    for copy in sends:
        copy.start()
    role_copies = [
        remote(meta, lists_v.at[0], 0, (ro, ri)),
        remote(positives.at[pl.ds(1, 2)], pos_role, 5, (ro, ri)),
        remote(negatives.at[pl.ds(1, 2)], neg_role, 6, (ro, ri)),
    ]
    own_copies = [
        pltpu.make_async_copy(meta, lists_v.at[0], local.at[6]),
        pltpu.make_async_copy(positives.at[pl.ds(1, 2)], pos_role, local.at[7]),
        pltpu.make_async_copy(negatives.at[pl.ds(1, 2)], neg_role, local.at[8]),
    ]

    @pl.when(stays)
    def _():
        for copy in own_copies:
            copy.start()

    @pl.when(jnp.logical_not(stays))
    def _():
        for copy in role_copies:
            copy.start()

    rows = lax.broadcasted_iota(jnp.int32, (TILE, TILE), 0)
    group = 2 if slots % 2 == 0 else 1
    width = pool0.shape[-1]

    def train(count, vert_at, prev_at, context_at, prevc_at, step, pos, neg, pool, held, cpool):
        def slot_group(g, carry):
            work = []
            for j in range(group):
                t = g * group + j
                live = (t < count).astype(jnp.float32)
                work.append((t, vert_at(t), context_at(t), live))
            anchors = [halves(pool[w[1]]) for w in work]
            partners = [halves(cpool[w[2]]) for w in work]
            gradients = []
            for (t, _, _, live), (a_high, a_low), (p_high, p_low) in zip(work, anchors, partners):
                both = jnp.concatenate([a_high, a_low], 1)
                twice = jnp.concatenate([p_high, p_high], 1)
                scores = dot(twice, both, ((1,), (1,))) + dot(p_low, a_high, ((1,), (1,)))
                half = -0.5 * learn_rate * live
                change = half * jnp.tanh(0.5 * scores) + half
                gradient = jnp.where(pos[step, pl.ds(t, 1)] == rows, change + learn_rate * live, 0.0)
                for k in range(neg.shape[2]):
                    gradient += jnp.where(neg[step, t, pl.ds(k, 1)] == rows, change, 0.0)
                gradients.append(halves(gradient))
            for (t, at_v, at_c, _), (a_high, a_low), (p_high, p_low), (g_high, g_low) in zip(
                work, anchors, partners, gradients
            ):
                wide = dot(g_high, jnp.concatenate([p_high, p_low], 1), ((0,), (0,)))
                prev = prev_at(t)
                base = pool[jnp.where(prev < 0, at_v, held + prev)]
                pool[held + t] = base + (wide[:, :width] + wide[:, width:] + dot(g_low, p_high, ((0,), (0,))))
                wide = dot(g_high, jnp.concatenate([a_high, a_low], 1), ((1,), (0,)))
                prev = prevc_at(t)
                base = cpool[jnp.where(prev < 0, at_c, ctiles + prev)]
                cpool[ctiles + t] = base + (wide[:, :width] + wide[:, width:] + dot(g_low, a_high, ((1,), (0,))))
            return carry

        lax.fori_loop(0, slots // group, slot_group, 0)

    def pack(source, targets, index):
        p = 0
        for target, size in targets:
            for k in range(size):
                target[k] = source[index(p)]
                p += 1

    def context_index(row):
        def index(k):
            slot = row(f.lastc + k)
            return jnp.where(slot < 0, k, ctiles + slot)
        return index

    def mine(s):
        return lambda k: meta_s[s, k]

    def other(which, s):
        return lambda k: lists[which, s, k]

    own_meta.wait()
    for copy in here[:4]:
        copy.wait()
    m = mine(0)
    train(
        m(f.count), lambda t: m(f.vert + t), lambda t: m(f.prev + t), lambda t: m(f.context + t),
        lambda t: m(f.prevc + t), 0, pos_home, neg_home, pool0, tiles, cpool0,
    )
    for copy in sends:
        copy.wait()

    @pl.when(stays)
    def _():
        for copy in own_copies:
            copy.wait()

    @pl.when(jnp.logical_not(stays))
    def _():
        for copy in role_copies:
            copy.wait()

    to_smem = pltpu.make_async_copy(lists_v, lists, local.at[9])
    to_smem.start()
    to_smem.wait()

    after = other(1, 1)

    def index0(p):
        tile = after(f.order + p)
        slot = m(f.last + tile)
        return jnp.where(slot < 0, tile, tiles + slot)

    pack(pool0, ((near0, slots),), index0)
    send_near0 = remote(near0, pool1.at[pl.ds(0, slots)], 7, swapped(*at(o, i + 1)))
    send_near0.start()
    pack(cpool0, ((csend0, ctiles),), context_index(m))
    send_c0 = remote(csend0, cpool1.at[pl.ds(0, ctiles)], 8, (ro, ri))
    keep_c0 = pltpu.make_async_copy(csend0, cpool1.at[pl.ds(0, ctiles)], local.at[10])

    @pl.when(stays)
    def _():
        keep_c0.start()

    @pl.when(jnp.logical_not(stays))
    def _():
        send_c0.start()

    pack(pool0, ((far0, tiles - slots),), lambda p: index0(slots + p))
    rest2 = pool2.at[pl.ds(slots, tiles - slots)]
    send_far0 = remote(far0, rest2, 9, at(o, i + 2))
    far0_a = remote(far0, relay_a, 15, at(o, i + 2))
    far0_b = remote(far0, relay_b, 16, (ro, ri))
    pass_a = remote(relay_a, rest2, 17, (ro, ri), 9)
    pass_b = remote(relay_b, rest2, 18, at(o, i + 2), 9)

    @when((0, 0))
    def _():
        send_far0.start()

    @when((1, 0))
    def _():
        far0_a.start()

    @when((0, 1))
    def _():
        far0_b.start()

    send_near0.wait()

    @pl.when(stays)
    def _():
        keep_c0.wait()

    @pl.when(jnp.logical_not(stays))
    def _():
        send_c0.wait()

    r = other(0, 1)
    train(
        r(f.count), lambda t: r(f.spot + t), lambda t: r(f.prev + t), lambda t: r(f.context + t),
        lambda t: r(f.prevc + t), 0, pos_role, neg_role, pool1, slots, cpool1,
    )

    def index1(p):
        slot = r(f.lastspot + p)
        return jnp.where(slot < 0, p, slots + slot)

    pack(pool1, ((near1, slots),), index1)
    send_near1 = remote(near1, pool2.at[pl.ds(0, slots)], 10, swapped(*at(ro, ri + 1)))
    send_near1.start()

    @when((1, 1))
    def _():
        send_far0.start()

    @when((1, 0))
    def _():
        far0_a.wait_recv()
        pass_a.start()
        far0_b.wait_recv()
        pass_b.start()

    pack(cpool1, ((cpool2, ctiles),), context_index(r))

    send_near1.wait()
    send_far0.wait_recv()
    r2 = other(0, 2)
    before = other(2, 1)
    train(
        r2(f.count), lambda t: before(f.place + r2(f.vert + t)), lambda t: r2(f.prev + t),
        lambda t: r2(f.context + t), lambda t: r2(f.prevc + t), 1, pos_role, neg_role, pool2, tiles, cpool2,
    )
    following = other(3, 3)

    def index2(p):
        tile = following(f.order + p)
        slot = r2(f.last + tile)
        return jnp.where(slot < 0, before(f.place + tile), tiles + slot)

    pack(pool2, ((near2, slots),), index2)
    send_near2 = remote(near2, pool3.at[pl.ds(0, slots)], 11, at(ro, ri + 1))
    send_near2.start()
    pack(cpool2, ((csend2, ctiles),), context_index(r2))
    send_c2 = remote(csend2, cpool3.at[pl.ds(0, ctiles)], 12, (ro, ri))
    keep_c2 = pltpu.make_async_copy(csend2, cpool3.at[pl.ds(0, ctiles)], local.at[11])

    @pl.when(stays)
    def _():
        keep_c2.start()

    @pl.when(jnp.logical_not(stays))
    def _():
        send_c2.start()

    pack(pool2, ((far2, tiles - slots),), lambda p: index2(slots + p))
    rest3 = last.at[pl.ds(slots, tiles - slots)]
    send_far2 = remote(far2, rest3, 13, at(ro + 1, ri + 1))
    far2_c = remote(far2, relay_c, 19, at(o + 2, i))
    pass_c = remote(relay_c, rest3, 20, at(o - 1, i + 1), 13)

    @when((1, 1))
    def _():
        far2_c.start()

    @when((0, 0), (0, 1), (1, 0))
    def _():
        send_far2.start()

    for copy in here[4:]:
        copy.wait()
    send_near2.wait()

    @pl.when(stays)
    def _():
        keep_c2.wait()

    @pl.when(jnp.logical_not(stays))
    def _():
        send_c2.wait()

    m3 = mine(3)
    train(
        m3(f.count), lambda t: m3(f.spot + t), lambda t: m3(f.prev + t), lambda t: m3(f.context + t),
        lambda t: m3(f.prevc + t), 1, pos_home, neg_home, pool3, slots, cpool3,
    )

    def index3(p):
        slot = m3(f.lastspot + p)
        return jnp.where(slot < 0, p, slots + slot)

    pack(pool3, ((near3, slots),), index3)
    send_near3 = remote(near3, last.at[pl.ds(0, slots)], 14, at(o + 1, i))
    send_near3.start()
    pack(cpool3, ((csend0, ctiles),), context_index(m3))
    put_c = pltpu.make_async_copy(csend0, c_out, local.at[12])
    put_c.start()

    @when((1, 1))
    def _():
        far2_c.wait_recv()
        pass_c.start()

    send_far2.wait_recv()
    send_near3.wait()

    @when((0, 0), (1, 1))
    def _():
        send_far0.wait_send()

    @when((1, 0))
    def _():
        far0_a.wait_send()
        pass_a.wait_send()
        pass_b.wait_send()

    @when((0, 1))
    def _():
        far0_b.wait_send()

    @when((0, 0), (0, 1), (1, 0))
    def _():
        send_far2.wait_send()

    @when((1, 1))
    def _():
        far2_c.wait_send()
        pass_c.wait_send()

    final = other(4, 3)
    pack(last, ((out, tiles),), lambda k: final(f.place + k))
    put_v = pltpu.make_async_copy(out, v_out, local.at[13])
    put_v.start()
    put_c.wait()
    put_v.wait()


ANY = pl.BlockSpec(memory_space=pl.ANY)
SMEM = pl.BlockSpec(memory_space=pltpu.SMEM)
VMEM = pl.BlockSpec(memory_space=pltpu.VMEM)


def body(vertex, context, tile_count, tile_vert, tile_context, positives, negatives):
    steps, slots = tile_vert.shape
    width = vertex.shape[1]
    tiles, ctiles = vertex.shape[0] // TILE, context.shape[0] // TILE
    f32, i32 = jnp.float32, jnp.int32
    meta = (-(-steps // 8) * 8, Fields(tiles, slots, ctiles).width)
    v = vertex.reshape(tiles, TILE, width)
    c = context.reshape(ctiles, TILE, width)

    def block(n):
        return pltpu.VMEM((n, TILE, width), f32)

    far = tiles - slots
    scratch = [
        block(tiles + slots), block(2 * slots), block(tiles + slots), block(2 * slots),
        *[block(ctiles + slots)] * 4,
        block(slots), block(far), block(slots), block(slots), block(far), block(slots),
        block(ctiles), block(ctiles), block(tiles), block(tiles),
        block(far), block(far), block(far),
        pltpu.VMEM(tile_vert.shape, i32), pltpu.VMEM(tile_context.shape, i32),
        pltpu.VMEM(meta, i32), pltpu.SMEM(meta, i32),
        pltpu.VMEM((5,) + meta, i32), pltpu.SMEM((5,) + meta, i32),
        *[pltpu.VMEM((2,) + positives.shape[1:], i32), pltpu.VMEM((2,) + negatives.shape[1:], i32)] * 2,
        pltpu.SemaphoreType.DMA((21,)), pltpu.SemaphoreType.DMA((21,)), pltpu.SemaphoreType.DMA((17,)),
    ]
    v, c = pl.pallas_call(
        functools.partial(kernel, (tiles, slots, ctiles)),
        out_shape=(jax.ShapeDtypeStruct(v.shape, f32), jax.ShapeDtypeStruct(c.shape, f32)),
        in_specs=[SMEM] + [ANY] * 6,
        out_specs=(ANY, ANY),
        scratch_shapes=scratch,
        compiler_params=pltpu.CompilerParams(collective_id=0, has_side_effects=True, vmem_limit_bytes=50 * 1024 * 1024),
    )(tile_count, tile_vert, tile_context, v, c, positives, negatives)
    return v.reshape(vertex.shape), c.reshape(context.shape)


def solution(mesh):
    lists = P(("outer", "inner"))
    rows = P(("outer", "inner"), None)
    return jax.shard_map(
        body,
        mesh=mesh,
        in_specs=(
            rows, rows, lists, rows, rows,
            P(("outer", "inner"), None, None), P(("outer", "inner"), None, None, None),
        ),
        out_specs=(rows, rows),
        check_vma=False,
    )
```

```python
import functools

import jax
import jax.numpy as jnp
from jax import lax
from jax.experimental import pallas as pl
from jax.experimental.pallas import tpu as pltpu
from jax.sharding import PartitionSpec as P

TILE = 256

learn_rate = 0.5

MESH = pl.DeviceIdType.MESH


def halves(x):
    high = x.astype(jnp.bfloat16)
    low = (x - high.astype(jnp.float32)).astype(jnp.bfloat16)
    return high, low


def dot(a, b, dims):
    return lax.dot_general(a, b, (dims, ((), ())), preferred_element_type=jnp.float32)


class Fields:
    def __init__(self, tiles, slots, ctiles):
        start = 0
        for name, size in (
            ("place", tiles), ("order", tiles), ("last", tiles), ("spot", slots), ("prev", slots),
            ("lastspot", slots), ("vert", slots), ("context", slots), ("prevc", slots),
            ("lastc", ctiles), ("count", 1),
        ):
            setattr(self, name, start)
            start += size
        self.width = -(-start // 128) * 128


def tables(f, tiles, slots, ctiles, count, vert, context):
    steps = vert.shape[0]
    shape = (steps, f.width)
    col = lax.broadcasted_iota(jnp.int32, shape, 1)
    row = lax.broadcasted_iota(jnp.int32, shape, 0)
    v = [jnp.broadcast_to(vert[:, t : t + 1], shape) for t in range(slots)]
    c = [jnp.broadcast_to(context[:, t : t + 1], shape) for t in range(slots)]

    def latest(values, at, upto=slots):
        found = jnp.full(shape, -1, jnp.int32)
        for t in range(upto):
            found = jnp.where(values[t] == at, t, found)
        return found

    first = [jnp.where(latest(v, v[t], t) < 0, 1, 0) for t in range(slots)]
    total = functools.reduce(lambda x, y: x + y, first)

    def before(at):
        return functools.reduce(lambda x, y: x + y, [jnp.where(v[t] < at, first[t], 0) for t in range(slots)])

    def place(at):
        count_before = before(at)
        return jnp.where(latest(v, at) >= 0, count_before, total + at - count_before)

    order = jnp.zeros(shape, jnp.int32)
    for k in range(tiles):
        order = jnp.where(place(jnp.full(shape, k, jnp.int32)) == col - f.order, k, order)
    out = jnp.zeros(shape, jnp.int32)

    def put(start, size, value):
        return jnp.where((col >= start) & (col < start + size), value, out)

    out = put(f.place, tiles, place(col - f.place))
    out = put(f.order, tiles, order)
    out = put(f.last, tiles, latest(v, col - f.last))
    spots = [before(v[t]) for t in range(slots)]
    out = put(f.lastspot, slots, latest(spots, col - f.lastspot))
    out = put(f.lastc, ctiles, latest(c, col - f.lastc))
    for t in range(slots):
        out = put(f.spot + t, 1, spots[t])
        out = put(f.prev + t, 1, latest(v, v[t], t))
        out = put(f.prevc + t, 1, latest(c, c[t], t))
        out = put(f.vert + t, 1, v[t])
        out = put(f.context + t, 1, c[t])
    for s in range(steps):
        out = jnp.where((row == s) & (col == f.count), count[s], out)
    return out


def kernel(
    sizes, tile_count, tile_vert, tile_context, vertex, context, positives, negatives, v_out, c_out,
    pool0, pool1, pool2, pool3, cpool0, cpool1, cpool2, cpool3,
    idle0, busy0, relay_idle, relay_busy, near1, rest1, rest, near2, far2, relay_c, near3, csend0, csend2, last, out,
    vert_v, context_v, meta, meta_s, lists_v, lists, pos_home, neg_home, pos_role, neg_role, send, recv, local,
):
    tiles, slots, ctiles = sizes
    f = Fields(tiles, slots, ctiles)
    outer, inner = lax.axis_size("outer"), lax.axis_size("inner")
    o, i = lax.axis_index("outer"), lax.axis_index("inner")

    def swapped(o, i):
        return 2 * (o // 2) + i % 2, 2 * (i // 2) + o % 2

    def at(o, i):
        return (o + outer) % outer, (i + inner) % inner

    ro, ri = swapped(o, i)
    stays = o % 2 == i % 2

    pair = (o % 2, i % 2)

    def when(*kinds):
        ok = [(pair[0] == a) & (pair[1] == b) for a, b in kinds]
        return pl.when(functools.reduce(jnp.logical_or, ok))

    def remote(source, target, k, device, into=None):
        return pltpu.make_async_remote_copy(
            src_ref=source, dst_ref=target, send_sem=send.at[k], recv_sem=recv.at[k if into is None else into],
            device_id=device, device_id_type=MESH,
        )

    load = [
        pltpu.make_async_copy(tile_vert, vert_v, local.at[14]),
        pltpu.make_async_copy(tile_context, context_v, local.at[15]),
    ]
    for copy in load:
        copy.start()

    here = [
        pltpu.make_async_copy(vertex, pool0.at[pl.ds(0, tiles)], local.at[0]),
        pltpu.make_async_copy(context, cpool0.at[pl.ds(0, ctiles)], local.at[1]),
        pltpu.make_async_copy(positives.at[pl.ds(0, 1)], pos_home.at[pl.ds(0, 1)], local.at[2]),
        pltpu.make_async_copy(negatives.at[pl.ds(0, 1)], neg_home.at[pl.ds(0, 1)], local.at[3]),
        pltpu.make_async_copy(positives.at[pl.ds(3, 1)], pos_home.at[pl.ds(1, 1)], local.at[4]),
        pltpu.make_async_copy(negatives.at[pl.ds(3, 1)], neg_home.at[pl.ds(1, 1)], local.at[5]),
    ]
    for copy in here:
        copy.start()

    barrier = pltpu.get_barrier_semaphore()
    sources = [
        at(o, i + 1), (ro, ri - 1), (ro, ri + 1), at(o - 1, i), swapped(*at(ro, ri - 1)),
        swapped(*at(o, i - 1)), swapped(*at(o - 1, i - 1)), at(o - 2, i),
    ]
    for source in sources:
        pl.semaphore_signal(barrier, inc=1, device_id=at(*source), device_id_type=MESH)

    @pl.when(jnp.logical_not(stays))
    def _():
        pl.semaphore_signal(barrier, inc=1, device_id=(ro, ri), device_id_type=MESH)

    for copy in load:
        copy.wait()
    meta[...] = jnp.zeros_like(meta)
    meta[pl.ds(0, vert_v.shape[0])] = tables(f, tiles, slots, ctiles, tile_count, vert_v, context_v)
    own_meta = pltpu.make_async_copy(meta, meta_s, local.at[16])
    own_meta.start()

    @pl.when(stays)
    def _():
        pl.semaphore_wait(barrier, len(sources))

    @pl.when(jnp.logical_not(stays))
    def _():
        pl.semaphore_wait(barrier, len(sources) + 1)

    sends = [
        remote(meta, lists_v.at[1], 1, swapped(*at(o, i + 1))),
        remote(meta, lists_v.at[2], 2, swapped(*at(o, i - 1))),
        remote(meta, lists_v.at[3], 3, at(o + 1, i)),
    ]
    for copy in sends:
        copy.start()
    role_copies = [
        remote(meta, lists_v.at[0], 0, (ro, ri)),
        remote(positives.at[pl.ds(1, 2)], pos_role, 5, (ro, ri)),
        remote(negatives.at[pl.ds(1, 2)], neg_role, 6, (ro, ri)),
    ]
    own_copies = [
        pltpu.make_async_copy(meta, lists_v.at[0], local.at[6]),
        pltpu.make_async_copy(positives.at[pl.ds(1, 2)], pos_role, local.at[7]),
        pltpu.make_async_copy(negatives.at[pl.ds(1, 2)], neg_role, local.at[8]),
    ]

    @pl.when(stays)
    def _():
        for copy in own_copies:
            copy.start()

    @pl.when(jnp.logical_not(stays))
    def _():
        for copy in role_copies:
            copy.start()

    rows = lax.broadcasted_iota(jnp.int32, (TILE, TILE), 0)
    group = 2 if slots % 2 == 0 else 1
    width = pool0.shape[-1]

    def train(count, vert_at, prev_at, context_at, prevc_at, step, pos, neg, pool, held, cpool):
        def slot_group(g, carry):
            work = []
            for j in range(group):
                t = g * group + j
                live = (t < count).astype(jnp.float32)
                work.append((t, vert_at(t), context_at(t), live))
            anchors = [halves(pool[w[1]]) for w in work]
            partners = [halves(cpool[w[2]]) for w in work]
            gradients = []
            for (t, _, _, live), (a_high, a_low), (p_high, p_low) in zip(work, anchors, partners):
                both = jnp.concatenate([a_high, a_low], 1)
                twice = jnp.concatenate([p_high, p_high], 1)
                scores = dot(twice, both, ((1,), (1,))) + dot(p_low, a_high, ((1,), (1,)))
                half = -0.5 * learn_rate * live
                change = half * jnp.tanh(0.5 * scores) + half
                gradient = jnp.where(pos[step, pl.ds(t, 1)] == rows, change + learn_rate * live, 0.0)
                for k in range(neg.shape[2]):
                    gradient += jnp.where(neg[step, t, pl.ds(k, 1)] == rows, change, 0.0)
                gradients.append(halves(gradient))
            for (t, at_v, at_c, _), (a_high, a_low), (p_high, p_low), (g_high, g_low) in zip(
                work, anchors, partners, gradients
            ):
                wide = dot(g_high, jnp.concatenate([p_high, p_low], 1), ((0,), (0,)))
                prev = prev_at(t)
                base = pool[jnp.where(prev < 0, at_v, held + prev)]
                pool[held + t] = base + (wide[:, :width] + wide[:, width:] + dot(g_low, p_high, ((0,), (0,))))
                wide = dot(g_high, jnp.concatenate([a_high, a_low], 1), ((1,), (0,)))
                prev = prevc_at(t)
                base = cpool[jnp.where(prev < 0, at_c, ctiles + prev)]
                cpool[ctiles + t] = base + (wide[:, :width] + wide[:, width:] + dot(g_low, a_high, ((1,), (0,))))
            return carry

        lax.fori_loop(0, slots // group, slot_group, 0)

    def pack(source, targets, index):
        p = 0
        for target, size in targets:
            for k in range(size):
                target[k] = source[index(p)]
                p += 1

    def context_index(row):
        def index(k):
            slot = row(f.lastc + k)
            return jnp.where(slot < 0, k, ctiles + slot)
        return index

    def mine(s):
        return lambda k: meta_s[s, k]

    def other(which, s):
        return lambda k: lists[which, s, k]

    def parts(n, most):
        count = most if n % most == 0 else 1
        return [(k * (n // count), n // count) for k in range(count)]

    far = tiles - slots
    idle_parts, busy_parts = parts(far, 2), parts(slots, 4)

    def moves(source, relay, start, pieces, k):
        direct, up, on = [], [], []
        for j, (begin, size) in enumerate(pieces):
            piece = pl.ds(begin, size)
            target = pool1.at[pl.ds(start + begin, size)]
            direct.append(remote(source.at[piece], target, k + j, swapped(*at(o, i + 1))))
            up.append(remote(source.at[piece], relay.at[piece], k + 6 + j, at(o, i - 1)))
            on.append(remote(relay.at[piece], target, k + 12 + j, at(o, i + 2), k + j))
        return direct, up, on

    idle_direct, idle_up, idle_on = moves(idle0, relay_idle, slots, idle_parts, 20)
    busy_direct, busy_up, busy_on = moves(busy0, relay_busy, 0, busy_parts, 22)
    straight = when((0, 0), (1, 0), (1, 1))

    def begin(copies):
        for copy in copies:
            copy.start()

    own_meta.wait()
    m = mine(0)
    here[0].wait()
    pack(pool0, ((idle0, far),), lambda p: m(f.order + slots + p))

    @straight
    def _():
        begin(idle_direct)

    @when((0, 1))
    def _():
        begin(idle_up)

    for copy in here[1:4]:
        copy.wait()
    train(
        m(f.count), lambda t: m(f.vert + t), lambda t: m(f.prev + t), lambda t: m(f.context + t),
        lambda t: m(f.prevc + t), 0, pos_home, neg_home, pool0, tiles, cpool0,
    )

    def index0(p):
        tile = m(f.order + p)
        slot = m(f.last + tile)
        return jnp.where(slot < 0, tile, tiles + slot)

    for j, (start, size) in enumerate(busy_parts):
        for p in range(start, start + size):
            busy0[p] = pool0[index0(p)]

        @straight
        def _():
            busy_direct[j].start()

    pack(cpool0, ((csend0, ctiles),), context_index(m))
    send_c0 = remote(csend0, cpool1.at[pl.ds(0, ctiles)], 8, (ro, ri))
    keep_c0 = pltpu.make_async_copy(csend0, cpool1.at[pl.ds(0, ctiles)], local.at[10])

    @pl.when(stays)
    def _():
        keep_c0.start()

    @pl.when(jnp.logical_not(stays))
    def _():
        send_c0.start()

    @when((0, 1))
    def _():
        begin(busy_up)

    for copy in sends:
        copy.wait()

    @pl.when(stays)
    def _():
        for copy in own_copies:
            copy.wait()

    @pl.when(jnp.logical_not(stays))
    def _():
        for copy in role_copies:
            copy.wait()

    to_smem = pltpu.make_async_copy(lists_v, lists, local.at[9])
    to_smem.start()

    @when((0, 0))
    def _():
        for arrived, passed in zip(idle_up + busy_up, idle_on + busy_on):
            arrived.wait_recv()
            passed.start()

    to_smem.wait()

    for copy in idle_direct + busy_direct:
        copy.wait_recv()

    @pl.when(stays)
    def _():
        keep_c0.wait()

    @pl.when(jnp.logical_not(stays))
    def _():
        send_c0.wait()

    r = other(0, 1)
    before = other(1, 0)
    train(
        r(f.count), lambda t: before(f.place + r(f.vert + t)), lambda t: r(f.prev + t),
        lambda t: r(f.context + t), lambda t: r(f.prevc + t), 0, pos_role, neg_role, pool1, tiles, cpool1,
    )
    second = other(2, 2)

    def index1(p):
        tile = second(f.order + p)
        slot = r(f.last + tile)
        return jnp.where(slot < 0, before(f.place + tile), tiles + slot)

    pack(pool1, ((near1, slots),), index1)
    send_near1 = remote(near1, pool2.at[pl.ds(0, slots)], 10, swapped(*at(ro, ri + 1)))
    send_near1.start()
    pack(pool1, ((rest1, far),), lambda p: index1(slots + p))
    send_rest1 = remote(rest1, rest, 9, swapped(*at(ro, ri + 1)))
    send_rest1.start()
    pack(cpool1, ((cpool2, ctiles),), context_index(r))

    send_near1.wait()
    r2 = other(0, 2)
    train(
        r2(f.count), lambda t: r2(f.spot + t), lambda t: r2(f.prev + t),
        lambda t: r2(f.context + t), lambda t: r2(f.prevc + t), 1, pos_role, neg_role, pool2, tiles, cpool2,
    )
    following = other(2, 3)

    def index2(p):
        tile = following(f.order + p)
        slot = r2(f.last + tile)
        return jnp.where(slot < 0, r2(f.place + tile), tiles + slot)

    send_rest1.wait()
    for k in range(far):
        pool2[slots + k] = rest[k]
    pack(pool2, ((near2, slots),), index2)
    send_near2 = remote(near2, pool3.at[pl.ds(0, slots)], 11, at(ro, ri + 1))
    send_near2.start()
    pack(cpool2, ((csend2, ctiles),), context_index(r2))
    send_c2 = remote(csend2, cpool3.at[pl.ds(0, ctiles)], 12, (ro, ri))
    keep_c2 = pltpu.make_async_copy(csend2, cpool3.at[pl.ds(0, ctiles)], local.at[11])

    @pl.when(stays)
    def _():
        keep_c2.start()

    @pl.when(jnp.logical_not(stays))
    def _():
        send_c2.start()

    pack(pool2, ((far2, far),), lambda p: index2(slots + p))
    rest3 = last.at[pl.ds(slots, tiles - slots)]
    send_far2 = remote(far2, rest3, 13, at(ro + 1, ri + 1))
    far2_c = remote(far2, relay_c, 14, at(o + 2, i))
    pass_c = remote(relay_c, rest3, 15, at(o - 1, i + 1), 13)

    @when((1, 1))
    def _():
        far2_c.start()

    @when((0, 0), (0, 1), (1, 0))
    def _():
        send_far2.start()

    for copy in here[4:]:
        copy.wait()
    send_near2.wait()

    @pl.when(stays)
    def _():
        keep_c2.wait()

    @pl.when(jnp.logical_not(stays))
    def _():
        send_c2.wait()

    m3 = mine(3)
    train(
        m3(f.count), lambda t: m3(f.spot + t), lambda t: m3(f.prev + t), lambda t: m3(f.context + t),
        lambda t: m3(f.prevc + t), 1, pos_home, neg_home, pool3, slots, cpool3,
    )

    def index3(p):
        slot = m3(f.lastspot + p)
        return jnp.where(slot < 0, p, slots + slot)

    pack(pool3, ((near3, slots),), index3)
    send_near3 = remote(near3, last.at[pl.ds(0, slots)], 16, at(o + 1, i))
    send_near3.start()
    pack(cpool3, ((csend0, ctiles),), context_index(m3))
    put_c = pltpu.make_async_copy(csend0, c_out, local.at[12])
    put_c.start()

    @when((1, 1))
    def _():
        far2_c.wait_recv()
        pass_c.start()

    send_far2.wait_recv()
    send_near3.wait()

    @straight
    def _():
        for copy in idle_direct + busy_direct:
            copy.wait_send()

    @when((0, 1))
    def _():
        for copy in idle_up + busy_up:
            copy.wait_send()

    @when((0, 0))
    def _():
        for copy in idle_on + busy_on:
            copy.wait_send()

    @when((0, 0), (0, 1), (1, 0))
    def _():
        send_far2.wait_send()

    @when((1, 1))
    def _():
        far2_c.wait_send()
        pass_c.wait_send()

    final = other(3, 3)
    pack(last, ((out, tiles),), lambda k: final(f.place + k))
    put_v = pltpu.make_async_copy(out, v_out, local.at[13])
    put_v.start()
    put_c.wait()
    put_v.wait()


HBM = pl.BlockSpec(memory_space=pltpu.HBM)
SMEM = pl.BlockSpec(memory_space=pltpu.SMEM)
VMEM = pl.BlockSpec(memory_space=pltpu.VMEM)


def body(vertex, context, tile_count, tile_vert, tile_context, positives, negatives):
    steps, slots = tile_vert.shape
    width = vertex.shape[1]
    tiles, ctiles = vertex.shape[0] // TILE, context.shape[0] // TILE
    f32, i32 = jnp.float32, jnp.int32
    meta = (-(-steps // 8) * 8, Fields(tiles, slots, ctiles).width)
    v = vertex.reshape(tiles, TILE, width)
    c = context.reshape(ctiles, TILE, width)

    def block(n):
        return pltpu.VMEM((n, TILE, width), f32)

    far = tiles - slots
    scratch = [
        block(tiles + slots), block(tiles + slots), block(tiles + slots), block(2 * slots),
        *[block(ctiles + slots)] * 4,
        block(far), block(slots), block(far), block(slots), block(slots), block(far), block(far),
        block(slots), block(far), block(far), block(slots),
        block(ctiles), block(ctiles), block(tiles), block(tiles),
        pltpu.VMEM(tile_vert.shape, i32), pltpu.VMEM(tile_context.shape, i32),
        pltpu.VMEM(meta, i32), pltpu.SMEM(meta, i32),
        pltpu.VMEM((4,) + meta, i32), pltpu.SMEM((4,) + meta, i32),
        *[pltpu.VMEM((2,) + positives.shape[1:], i32), pltpu.VMEM((2,) + negatives.shape[1:], i32)] * 2,
        pltpu.SemaphoreType.DMA((40,)), pltpu.SemaphoreType.DMA((40,)), pltpu.SemaphoreType.DMA((17,)),
    ]
    v, c = pl.pallas_call(
        functools.partial(kernel, (tiles, slots, ctiles)),
        out_shape=(jax.ShapeDtypeStruct(v.shape, f32), jax.ShapeDtypeStruct(c.shape, f32)),
        in_specs=[SMEM] + [HBM] * 6,
        out_specs=(HBM, HBM),
        scratch_shapes=scratch,
        compiler_params=pltpu.CompilerParams(collective_id=0, has_side_effects=True, vmem_limit_bytes=67_043_328),
    )(tile_count, tile_vert, tile_context, v, c, positives, negatives)
    return v.reshape(vertex.shape), c.reshape(context.shape)


def solution(mesh):
    lists = P(("outer", "inner"))
    rows = P(("outer", "inner"), None)
    return jax.shard_map(
        body,
        mesh=mesh,
        in_specs=(
            rows, rows, lists, rows, rows,
            P(("outer", "inner"), None, None), P(("outer", "inner"), None, None, None),
        ),
        out_specs=(rows, rows),
        check_vma=False,
    )
```
